256 devices in a mesh: param: 32 (over y, x, core), walker: 8 (over z).
Axes of the slice: x: 4, y: 4, z: 8, core: 2. Of those that a mesh axis runs over, the one named last changes fastest.
Arguments:
- derivs: float32 [64, 4980736], P('walker', 'param'), may hold values from -1.7 to 1.7
- gradient: float32 [4980736], P('param'), may hold values from -0.01171875 to 0.01171875
Outputs:
- solution: float32 [4980736], P(('param', 'walker'))
The draws below stay inside these ranges and needn't reach their ends.
All inputs are finite; a program needn't handle non-finite values.
Results may differ from the reference program's by a relative error of at most 0.0003.
Values sent between devices are 32-bit elements; how exact they have to be, the bound alone decides.
A program may use at most 64 MiB of HBM per device.

```python
import math
import jax
import jax.numpy as jnp
from jax import lax

P_SIZE = 4980736
ITERS = 3
ROWS = 64


def draw_derivs(key, part):
    key_vals, key_cols, key_rows = jax.random.split(key, 3)
    col_scale = jnp.exp(jax.random.uniform(key_cols, (P_SIZE,), jnp.float32, math.log(0.3), math.log(3.0)))
    ramp = 1.0 + 2.0 * jnp.arange(ROWS, dtype=jnp.float32) / (ROWS - 1)
    row_scale = ramp * jnp.exp(jax.random.uniform(key_rows, (ROWS,), jnp.float32, math.log(0.5), math.log(1.5)))
    values = jax.random.truncated_normal(key_vals, -4.0, 4.0, (ROWS, P_SIZE), jnp.float32)
    return (0.03 * row_scale[:, None] * col_scale[None, :] * values).astype(jnp.float32)


def block_levels(own_key, shape, shards, least, top_value):
    gain = 1.0
    for dim, parts in shards:
        heights = jax.random.uniform(jax.random.fold_in(jax.random.fold_in(own_key, 6), dim), (parts,), jnp.float32, least / len(shards), top_value / len(shards))
        gain = gain * jnp.repeat(jnp.exp(heights), shape[dim] // parts).reshape((-1,) + (1,) * (len(shape) - 1 - dim))
    return gain


def bell_draw(rng, dims, deviation, bound, cuts=(), kind=jnp.bfloat16):
    entries = jax.random.normal(rng, dims, jnp.float32) * deviation
    if len(cuts) > 0:
        entries = block_levels(rng, dims, cuts, -0.22, 0.18) * entries
    return jnp.clip(entries, min=-bound, max=bound).astype(kind)


def setup_inputs(seed: int = 0) -> dict:
    arg_keys = jax.random.split(jax.random.key(seed), 3)
    return {
        "derivs": draw_derivs(jax.random.fold_in(arg_keys[2], 71), 0),
        "gradient": bell_draw(arg_keys[1], (P_SIZE,), 0.002, 0.01171875, ((0, 32),), jnp.float32),
    }


DAMPING = 0.001


def operate(derivs, vector):
    row_vals = jnp.dot(derivs, vector, precision=lax.Precision.HIGHEST)
    back_vals = jnp.dot(row_vals, derivs, precision=lax.Precision.HIGHEST)
    return back_vals / ROWS + DAMPING * vector


def reference(derivs, gradient):
    solution = jnp.zeros_like(gradient)
    residual = gradient
    direction = gradient
    norm_now = jnp.sum(residual * residual)
    for step_idx in range(ITERS):
        image = operate(derivs, direction)
        step_len = norm_now / jnp.sum(direction * image)
        solution = solution + step_len * direction
        residual = residual - step_len * image
        norm_next = jnp.sum(residual * residual)
        direction = residual + (norm_next / norm_now) * direction
        norm_now = norm_next
    return solution
```

```python
import functools

import jax
import jax.numpy as jnp
from jax import lax
from jax.experimental import pallas as pl
from jax.experimental.pallas import tpu as pltpu
from jax.sharding import PartitionSpec as P

DAMPING = 0.001
LANES = 128
MESH = pl.DeviceIdType.MESH


def kernel(cfg, d_hbm, g_hbm, x_ref, dv, gv, t1, t2, r1f, r2f, rb, acc,
           msg, gath, wbuf, zmsg, zgath,
           load_sem, ring_send, ring_recv, pl_send, pl_recv, z_send, z_recv):
    n_p, n_z, rows, sh, cut, rows_all = cfg
    me_p = lax.axis_index("param")
    me_z = lax.axis_index("walker")
    groups = sh // 8
    right = lax.rem(me_z + 1, n_z)
    left = lax.rem(me_z + n_z - 1, n_z)

    def base(k):
        return pl.multiple_of(lax.rem(me_z + (k + n_z), n_z) * sh, 8)

    barrier = pltpu.get_barrier_semaphore()

    def greet_p(i, c):
        pl.semaphore_signal(barrier, inc=1, device_id={"param": lax.rem(me_p + i, n_p)}, device_id_type=MESH)
        return c

    def greet_z(i, c):
        pl.semaphore_signal(barrier, inc=1, device_id={"walker": lax.rem(me_z + i, n_z)}, device_id_type=MESH)
        return c

    gcopy = pltpu.make_async_copy(g_hbm, gv, load_sem.at[n_z, 0])
    gcopy.start()
    loads = []
    for k in range(n_z):
        for r in range(rows):
            c = pltpu.make_async_copy(d_hbm.at[pl.ds(k * sh, sh), r, :], dv.at[r, pl.ds(k * sh, sh), :], load_sem.at[k, r])
            c.start()
            loads.append(c)
    lax.fori_loop(1, n_p, greet_p, 0)
    lax.fori_loop(1, n_z, greet_z, 0)

    def accum(b, vec, others, first):
        n = rows + 1 + len(others)
        if first:
            a = [jnp.zeros((8, LANES), jnp.float32) for _ in range(n)]
        else:
            a = [acc[i] for i in range(n)]

        def step(i, a):
            o = pl.multiple_of(b + i * 8, 8)
            v = vec[pl.ds(o, 8), :]
            out = [a[r] + dv[r, pl.ds(o, 8), :] * v for r in range(rows)]
            out.append(a[rows] + v * v)
            for j, ref in enumerate(others):
                out.append(a[rows + 1 + j] + ref[pl.ds(o, 8), :] * v)
            return tuple(out)

        a = lax.fori_loop(0, groups, step, tuple(a), unroll=True)
        for i in range(n):
            acc[i] = a[i]

    sub = lax.broadcasted_iota(jnp.int32, (16, LANES), 0)
    lane = lax.broadcasted_iota(jnp.int32, (16, LANES), 1)
    diag = sub == lane

    def plane_sum(it):
        part = jnp.sum(acc[...], axis=1)
        part = jnp.sum(part, axis=1, keepdims=True)
        row = jnp.sum(jnp.where(diag, part, 0.0), axis=0, keepdims=True)
        msg[it] = row
        gath[it, me_p] = row

        def send(i, c):
            peer = lax.rem(me_p + i, n_p)
            pltpu.make_async_remote_copy(msg.at[it], gath.at[it, me_p], pl_send.at[it], pl_recv.at[it],
                                         device_id={"param": peer}, device_id_type=MESH).start()
            return c

        lax.fori_loop(1, n_p, send, 0)
        every = gath.at[it, pl.ds(0, n_p - 1)]
        pltpu.make_async_copy(every, every, pl_recv.at[it]).wait()
        tot = jnp.sum(gath[it, :, 0, :], axis=0, keepdims=True)
        tot = jnp.sum(jnp.where(diag, tot, 0.0), axis=1, keepdims=True)
        return jnp.broadcast_to(tot, (16, LANES))

    def z_start(it, w):
        row = jnp.sum(w * w, axis=0, keepdims=True)
        zmsg[it] = row
        zgath[it, me_z] = row

        def send(i, c):
            peer = lax.rem(me_z + i, n_z)
            pltpu.make_async_remote_copy(zmsg.at[it], zgath.at[it, me_z], z_send.at[it], z_recv.at[it],
                                         device_id={"walker": peer}, device_id_type=MESH).start()
            return c

        lax.fori_loop(1, n_z, send, 0)

    def z_finish(it):
        every = zgath.at[it, pl.ds(0, n_z - 1)]
        pltpu.make_async_copy(every, every, z_recv.at[it]).wait()
        return jnp.sum(zgath[it, :, 0, :], axis=0, keepdims=True)

    def project(k, t, w):
        b = base(k)

        def step(i, c):
            o = pl.multiple_of(b + i * 8, 8)
            s = dv[0, pl.ds(o, 8), :] * w[0]
            for r in range(1, rows):
                s = s + dv[r, pl.ds(o, 8), :] * w[r]
            t[pl.ds(o, 8), :] = s
            return c

        lax.fori_loop(0, groups, step, 0, unroll=True)

    half = ((0, cut), (cut, sh - cut))

    def ring(it, phase, way, s, c, src, dst):
        return pltpu.make_async_remote_copy(
            src, dst, ring_send.at[it, phase, way, s, c], ring_recv.at[it, phase, way, s, c],
            device_id={"walker": right if way == 0 else left}, device_id_type=MESH)

    steps = n_z // 2

    def reduce_scatter(it, t, w):
        wv = [jnp.broadcast_to(w[r:r + 1, :], (8, LANES)) for r in range(rows)]
        sends = {}

        def send(way, s, c):
            sign = 1 if way == 0 else -1
            lo, n = half[c]
            b = base(sign * (steps - s))
            cp = ring(it, 0, way, s, c, t.at[pl.ds(b + lo, n), :], rb.at[it, way, s, pl.ds(lo, n), :])
            cp.start()
            sends[way, s, c] = cp

        def add(way, s, c):
            sends[way, s, c].wait_recv()
            sign = 1 if way == 0 else -1
            lo, n = half[c]
            b = pl.multiple_of(base(sign * (steps - s - 1)) + lo, 8)
            t[pl.ds(b, n), :] += rb[it, way, s, pl.ds(lo, n), :]

        project(steps, t, wv)
        send(0, 0, 0)
        send(1, 0, 1)
        project(steps - 1, t, wv)
        send(0, 1, 1)
        project(1 - steps, t, wv)
        send(1, 1, 0)
        for k in range(steps - 2, 0, -1):
            project(k, t, wv)
            project(-k, t, wv)
        project(0, t, wv)
        for s in range(1, steps):
            for way in range(2):
                add(way, s - 1, way)
                send(way, s, way)
            for way in range(2):
                add(way, s, 1 - way)
                if s + 1 < steps:
                    send(way, s + 1, 1 - way)
        for way in range(2):
            add(way, steps - 1, way)
        for cp in sends.values():
            cp.wait_send()

    def all_gather(it, rf, others):
        sends = {}

        def send(way, s, c):
            sign = 1 if way == 0 else -1
            lo, n = half[c]
            piece = rf.at[pl.ds(base(-sign * s) + lo, n), :]
            cp = ring(it, 1, way, s, c, piece, piece)
            cp.start()
            sends[way, s, c] = cp

        for way in range(2):
            send(way, 0, way)
        for way in range(2):
            send(way, 0, 1 - way)
        accum(base(0), rf, others, True)
        for s in range(steps):
            for way in range(2):
                sends[way, s, way].wait_recv()
                if s + 1 < steps:
                    send(way, s + 1, way)
            if s + 1 < steps:
                for way in range(2):
                    sends[way, s, 1 - way].wait_recv()
                    if s + 2 < steps:
                        send(way, s + 1, 1 - way)
                accum(base(-1 - s), rf, others, False)
                accum(base(1 + s), rf, others, False)
            else:
                accum(base(steps), rf, others, False)
        for cp in sends.values():
            cp.wait_send()

    own = pl.ds(base(0), sh)
    inv = 1.0 / rows_all

    acc[...] = jnp.zeros_like(acc)
    gcopy.wait()
    for k in range(n_z):
        for r in range(rows):
            loads[k * rows + r].wait()
        accum(k * sh, gv, (), k == 0)
    pl.semaphore_wait(barrier, n_p - 1 + n_z - 1)

    tot = plane_sum(0)
    w0, rr0 = tot[:rows], tot[rows:rows + 1]
    pp0 = rr0
    z_start(0, w0)
    reduce_scatter(0, t1, w0)
    a0 = rr0 / (z_finish(0) * inv + DAMPING * pp0)
    r1f[own, :] = gv[own, :] - a0 * (t1[own, :] * inv + DAMPING * gv[own, :])

    all_gather(0, r1f, (gv,))
    tot = plane_sum(1)
    rr1, rp1 = tot[rows:rows + 1], tot[rows + 1:rows + 2]
    b0 = rr1 / rr0
    u1 = tot[:rows]
    w1 = u1 + b0 * w0
    pp1 = rr1 + b0 * (2.0 * rp1 + b0 * pp0)
    z_start(1, w1)
    reduce_scatter(1, t2, u1)
    a1 = rr1 / (z_finish(1) * inv + DAMPING * pp1)
    p1 = r1f[own, :] + b0 * gv[own, :]
    r2f[own, :] = r1f[own, :] - a1 * ((t2[own, :] + b0 * t1[own, :]) * inv + DAMPING * p1)

    all_gather(1, r2f, (gv, r1f))
    tot = plane_sum(2)
    rr2, rg2, rq2 = tot[rows:rows + 1], tot[rows + 1:rows + 2], tot[rows + 2:rows + 3]
    b1 = rr2 / rr1
    w2 = tot[:rows] + b1 * w1
    pp2 = rr2 + b1 * (2.0 * (rq2 + b0 * rg2) + b1 * pp1)
    z_start(2, w2)
    a2 = rr2 / (z_finish(2) * inv + DAMPING * pp2)
    p1 = r1f[own, :] + b0 * gv[own, :]
    p2 = r2f[own, :] + b1 * p1
    x_ref[...] = a0 * gv[own, :] + a1 * p1 + a2 * p2

    for it in range(3):
        every = gath.at[it, pl.ds(0, n_p - 1)]
        pltpu.make_async_copy(every, every, pl_send.at[it]).wait()
        every = zgath.at[it, pl.ds(0, n_z - 1)]
        pltpu.make_async_copy(every, every, z_send.at[it]).wait()


def body(derivs, gradient):
    n_p, n_z = lax.axis_size("param"), lax.axis_size("walker")
    rows, cols = derivs.shape
    tiles = cols // LANES
    sh = tiles // n_z
    cut = (sh // 2 + 7) // 8 * 8
    d = derivs.reshape(rows, tiles, LANES).transpose(1, 0, 2)
    g = gradient.reshape(tiles, LANES)
    f32 = jnp.float32
    full = pltpu.VMEM((tiles, LANES), f32)
    steps = n_z // 2
    x = pl.pallas_call(
        functools.partial(kernel, (n_p, n_z, rows, sh, cut, rows * n_z)),
        out_shape=jax.ShapeDtypeStruct((sh, LANES), f32),
        in_specs=[pl.BlockSpec(memory_space=pltpu.HBM)] * 2,
        out_specs=pl.BlockSpec(memory_space=pltpu.VMEM),
        scratch_shapes=[
            pltpu.VMEM((rows, tiles, LANES), f32),
            full, full, full, full, full,
            pltpu.VMEM((2, 2, steps, sh, LANES), f32),
            pltpu.VMEM((16, 8, LANES), f32),
            pltpu.VMEM((3, 1, LANES), f32),
            pltpu.VMEM((3, n_p, 1, LANES), f32),
            pltpu.VMEM((16, LANES), f32),
            pltpu.VMEM((3, 1, LANES), f32),
            pltpu.VMEM((3, n_z, 1, LANES), f32),
            pltpu.SemaphoreType.DMA((n_z + 1, rows)),
            pltpu.SemaphoreType.DMA((2, 2, 2, steps, 2)),
            pltpu.SemaphoreType.DMA((2, 2, 2, steps, 2)),
            pltpu.SemaphoreType.DMA((3,)),
            pltpu.SemaphoreType.DMA((3,)),
            pltpu.SemaphoreType.DMA((3,)),
            pltpu.SemaphoreType.DMA((3,)),
        ],
        compiler_params=pltpu.CompilerParams(
            collective_id=0, has_side_effects=True, vmem_limit_bytes=40 * 1024 * 1024),
        name="cg_solve",
    )(d, g)
    return x.reshape(sh * LANES)


def solution(mesh):
    in_specs = (P("walker", "param"), P("param"))
    out_specs = P(("param", "walker"))
    return jax.shard_map(body, mesh=mesh, in_specs=in_specs, out_specs=out_specs, check_vma=False)
```

```python
import functools

import jax
import jax.numpy as jnp
from jax import lax
from jax.experimental import pallas as pl
from jax.experimental.pallas import tpu as pltpu
from jax.sharding import PartitionSpec as P

DAMPING = 0.001
PIECES = 4
LANES = 128
MESH = pl.DeviceIdType.MESH


def kernel(cfg, d_hbm, g_hbm, x_ref, dv, gv, t1, t2, r1f, r2f, rb, acc,
           msg, gath, zmsg, zgath,
           load_sem, ring_send, ring_recv, pl_send, pl_recv, z_send, z_recv):
    n_p, n_z, rows, sh, cuts, rows_all = cfg
    me_p = lax.axis_index("param")
    me_z = lax.axis_index("walker")
    groups = sh // 8

    def base(k):
        return pl.multiple_of(lax.rem(me_z + (k + n_z), n_z) * sh, 8)

    barrier = pltpu.get_barrier_semaphore()

    def greet_p(i, c):
        pl.semaphore_signal(barrier, inc=1, device_id={"param": lax.rem(me_p + i, n_p)}, device_id_type=MESH)
        return c

    def greet_z(i, c):
        pl.semaphore_signal(barrier, inc=1, device_id={"walker": lax.rem(me_z + i, n_z)}, device_id_type=MESH)
        return c

    lax.fori_loop(1, n_p, greet_p, 0)
    lax.fori_loop(1, n_z, greet_z, 0)

    gcopy = pltpu.make_async_copy(g_hbm, gv, load_sem.at[n_z, 0])
    gcopy.start()
    loads = []
    for k in range(n_z):
        for r in range(rows):
            c = pltpu.make_async_copy(d_hbm.at[pl.ds(k * sh, sh), r, :], dv.at[r, pl.ds(k * sh, sh), :], load_sem.at[k, r])
            c.start()
            loads.append(c)

    def accum(vec, others):
        n = rows + 1 + len(others)

        def shard(k, a):
            out = list(a)
            for i in range(groups):
                o = pl.multiple_of(k * sh + i * 8, 8)
                v = vec[pl.ds(o, 8), :]
                for r in range(rows):
                    out[r] = out[r] + dv[r, pl.ds(o, 8), :] * v
                out[rows] = out[rows] + v * v
                for j, ref in enumerate(others):
                    out[rows + 1 + j] = out[rows + 1 + j] + ref[pl.ds(o, 8), :] * v
            return tuple(out)

        a = lax.fori_loop(0, n_z, shard, tuple(jnp.zeros((8, LANES), jnp.float32) for _ in range(n)))
        for i in range(n):
            acc[i] = a[i]

    sub = lax.broadcasted_iota(jnp.int32, (16, LANES), 0)
    lane = lax.broadcasted_iota(jnp.int32, (16, LANES), 1)
    diag = sub == lane

    def plane_sum(it):
        part = jnp.sum(acc[...], axis=1)
        part = jnp.sum(part, axis=1, keepdims=True)
        row = jnp.sum(jnp.where(diag, part, 0.0), axis=0, keepdims=True)
        msg[it] = row
        gath[it, me_p] = row

        def send(i, c):
            peer = lax.rem(me_p + i, n_p)
            pltpu.make_async_remote_copy(msg.at[it], gath.at[it, me_p], pl_send.at[it], pl_recv.at[it],
                                         device_id={"param": peer}, device_id_type=MESH).start()
            return c

        lax.fori_loop(1, n_p, send, 0)
        every = gath.at[it, pl.ds(0, n_p - 1)]
        pltpu.make_async_copy(every, every, pl_recv.at[it]).wait()
        tot = jnp.sum(gath[it, :, 0, :], axis=0, keepdims=True)
        tot = jnp.sum(jnp.where(diag, tot, 0.0), axis=1, keepdims=True)
        return jnp.broadcast_to(tot, (16, LANES))

    def z_start(it, w):
        row = jnp.sum(w * w, axis=0, keepdims=True)
        zmsg[it] = row
        zgath[it, me_z] = row

        def send(i, c):
            peer = lax.rem(me_z + i, n_z)
            pltpu.make_async_remote_copy(zmsg.at[it], zgath.at[it, me_z], z_send.at[it], z_recv.at[it],
                                         device_id={"walker": peer}, device_id_type=MESH).start()
            return c

        lax.fori_loop(1, n_z, send, 0)

    def z_finish(it):
        every = zgath.at[it, pl.ds(0, n_z - 1)]
        pltpu.make_async_copy(every, every, z_recv.at[it]).wait()
        return jnp.sum(zgath[it, :, 0, :], axis=0, keepdims=True)

    def project(first, count, t, wv):
        def shard(k, c):
            b = base(first + k)
            for i in range(groups):
                o = pl.multiple_of(b + i * 8, 8)
                s = dv[0, pl.ds(o, 8), :] * wv[0]
                for r in range(1, rows):
                    s = s + dv[r, pl.ds(o, 8), :] * wv[r]
                t[pl.ds(o, 8), :] = s
            return c

        lax.fori_loop(0, count, shard, 0)

    pieces = tuple((cuts[c], cuts[c + 1] - cuts[c]) for c in range(len(cuts) - 1))
    n_c = len(pieces)
    far = (range(n_c // 2), range(n_c // 2, n_c))
    signs = (1, -1)

    def ring(it, phase, way, kind, c, hops, src, dst):
        return pltpu.make_async_remote_copy(
            src, dst, ring_send.at[it, phase], ring_recv.at[it, phase, way, kind, c],
            device_id={"walker": lax.rem(me_z + n_z + signs[way] * hops, n_z)}, device_id_type=MESH)

    def span(k, c):
        lo, n = pieces[c]
        return pl.ds(pl.multiple_of(base(k) + lo, 8), n)

    def reduce_scatter(it, t, w, finish):
        wv = [jnp.broadcast_to(w[r:r + 1, :], (8, LANES)) for r in range(rows)]

        def copy(way, kind, c, k, hops):
            lo, n = pieces[c]
            return ring(it, 0, way, kind, c, hops, t.at[span(signs[way] * k, c), :],
                        rb.at[it, way, kind, pl.ds(lo, n), :])

        def landed(way, kind, c):
            lo, n = pieces[c]
            return rb[it, way, kind, pl.ds(lo, n), :]

        project(3, 3, t, wv)
        for c in range(n_c):
            for way in range(2):
                if c in far[way]:
                    copy(way, 0, c, 4, 2).start()
            for way in range(2):
                copy(way, 1, c, 3, 1).start()
        project(6, 5, t, wv)
        for c in range(n_c):
            for way in range(2):
                copy(way, 2, c, 1, 1).start()
        for c in range(n_c):
            for way in range(2):
                copy(way, 1, c, 3, 1).wait_recv()
                s = landed(way, 1, c)
                if c in far[way]:
                    copy(way, 0, c, 4, 2).wait_recv()
                    s = s + landed(way, 0, c)
                t[span(signs[way] * 2, c), :] += s
                copy(way, 3, c, 2, 2).start()
        for c in range(n_c):
            s = t[span(0, c), :]
            for way in range(2):
                copy(way, 2, c, 1, 1).wait_recv()
                copy(way, 3, c, 2, 2).wait_recv()
                s = s + (landed(way, 2, c) + landed(way, 3, c))
            t[span(0, c), :] = s
            finish(c)

    def gather_copy(it, rf, way, kind, c, k, hops):
        piece = rf.at[span(-signs[way] * k, c), :]
        return ring(it, 1, way, kind, c, hops, piece, piece)

    def gather_start(it, rf, c):
        for way in range(2):
            gather_copy(it, rf, way, 0, c, 0, 2).start()
        for way in range(2):
            gather_copy(it, rf, way, 1, c, 0, 1).start()

    def gather_finish(it, rf):
        for c in range(n_c):
            for way in range(2):
                gather_copy(it, rf, way, 0, c, 0, 2).wait_recv()
                if c in far[way]:
                    gather_copy(it, rf, way, 3, c, 2, 2).start()
                gather_copy(it, rf, way, 2, c, 2, 1).start()
        for c in range(n_c):
            for way in range(2):
                gather_copy(it, rf, way, 1, c, 0, 1).wait_recv()
                gather_copy(it, rf, way, 2, c, 2, 1).wait_recv()
                if c in far[way]:
                    gather_copy(it, rf, way, 3, c, 2, 2).wait_recv()

    own = pl.ds(base(0), sh)
    inv = 1.0 / rows_all

    acc[...] = jnp.zeros_like(acc)
    gcopy.wait()
    for c in loads:
        c.wait()
    accum(gv, ())
    pl.semaphore_wait(barrier, n_p - 1 + n_z - 1)

    tot = plane_sum(0)
    w0, rr0 = tot[:rows], tot[rows:rows + 1]
    pp0 = rr0
    z_start(0, w0)
    a0 = []

    def residual1(c):
        if c == 0:
            a0.append(rr0 / (z_finish(0) * inv + DAMPING * pp0))
        at = span(0, c)
        r1f[at, :] = gv[at, :] - a0[0] * (t1[at, :] * inv + DAMPING * gv[at, :])
        gather_start(0, r1f, c)

    reduce_scatter(0, t1, w0, residual1)
    gather_finish(0, r1f)
    accum(r1f, (gv,))

    tot = plane_sum(1)
    rr1, rp1 = tot[rows:rows + 1], tot[rows + 1:rows + 2]
    b0 = rr1 / rr0
    u1 = tot[:rows]
    w1 = u1 + b0 * w0
    pp1 = rr1 + b0 * (2.0 * rp1 + b0 * pp0)
    z_start(1, w1)
    a1 = []

    def residual2(c):
        if c == 0:
            a1.append(rr1 / (z_finish(1) * inv + DAMPING * pp1))
        at = span(0, c)
        p1 = r1f[at, :] + b0 * gv[at, :]
        r2f[at, :] = r1f[at, :] - a1[0] * ((t2[at, :] + b0 * t1[at, :]) * inv + DAMPING * p1)
        gather_start(1, r2f, c)

    reduce_scatter(1, t2, u1, residual2)
    gather_finish(1, r2f)
    accum(r2f, (gv, r1f))

    tot = plane_sum(2)
    rr2, rg2, rq2 = tot[rows:rows + 1], tot[rows + 1:rows + 2], tot[rows + 2:rows + 3]
    b1 = rr2 / rr1
    w2 = tot[:rows] + b1 * w1
    pp2 = rr2 + b1 * (2.0 * (rq2 + b0 * rg2) + b1 * pp1)
    z_start(2, w2)
    p1 = r1f[own, :] + b0 * gv[own, :]
    x1 = a0[0] * gv[own, :] + a1[0] * p1
    p2 = r2f[own, :] + b1 * p1
    a2 = rr2 / (z_finish(2) * inv + DAMPING * pp2)
    x_ref[...] = x1 + a2 * p2

    sent = pl.ds(0, (n_z - 1) * sh)
    for it in range(2):
        for phase, ref in enumerate(((t1, t2)[it], (r1f, r2f)[it])):
            every = ref.at[sent, :]
            pltpu.make_async_copy(every, every, ring_send.at[it, phase]).wait()
    for it in range(3):
        every = gath.at[it, pl.ds(0, n_p - 1)]
        pltpu.make_async_copy(every, every, pl_send.at[it]).wait()
        every = zgath.at[it, pl.ds(0, n_z - 1)]
        pltpu.make_async_copy(every, every, z_send.at[it]).wait()


def body(derivs, gradient):
    n_p, n_z = lax.axis_size("param"), lax.axis_size("walker")
    rows, cols = derivs.shape
    tiles = cols // LANES
    sh = tiles // n_z
    cuts = tuple((sh // 8 * c + PIECES - 1) // PIECES * 8 for c in range(PIECES + 1))
    d = derivs.reshape(rows, tiles, LANES).transpose(1, 0, 2)
    g = gradient.reshape(tiles, LANES)
    f32 = jnp.float32
    full = pltpu.VMEM((tiles, LANES), f32)
    x = pl.pallas_call(
        functools.partial(kernel, (n_p, n_z, rows, sh, cuts, rows * n_z)),
        out_shape=jax.ShapeDtypeStruct((sh, LANES), f32),
        in_specs=[pl.BlockSpec(memory_space=pltpu.HBM)] * 2,
        out_specs=pl.BlockSpec(memory_space=pltpu.VMEM),
        scratch_shapes=[
            pltpu.VMEM((rows, tiles, LANES), f32),
            full, full, full, full, full,
            pltpu.VMEM((2, 2, 4, sh, LANES), f32),
            pltpu.VMEM((16, 8, LANES), f32),
            pltpu.VMEM((3, 1, LANES), f32),
            pltpu.VMEM((3, n_p, 1, LANES), f32),
            pltpu.VMEM((3, 1, LANES), f32),
            pltpu.VMEM((3, n_z, 1, LANES), f32),
            pltpu.SemaphoreType.DMA((n_z + 1, rows)),
            pltpu.SemaphoreType.DMA((2, 2)),
            pltpu.SemaphoreType.DMA((2, 2, 2, 4, PIECES)),
            pltpu.SemaphoreType.DMA((3,)),
            pltpu.SemaphoreType.DMA((3,)),
            pltpu.SemaphoreType.DMA((3,)),
            pltpu.SemaphoreType.DMA((3,)),
        ],
        compiler_params=pltpu.CompilerParams(
            collective_id=0, has_side_effects=True, vmem_limit_bytes=56 * 1024 * 1024),
        name="cg_solve",
    )(d, g)
    return x.reshape(sh * LANES)


def solution(mesh):
    in_specs = (P("walker", "param"), P("param"))
    out_specs = P(("param", "walker"))
    return jax.shard_map(body, mesh=mesh, in_specs=in_specs, out_specs=out_specs, check_vma=False)
```

```python
import functools

import jax
import jax.numpy as jnp
from jax import lax
from jax.experimental import pallas as pl
from jax.experimental.pallas import tpu as pltpu
from jax.sharding import PartitionSpec as P

DAMPING = 0.001
PIECES = 4
AHEAD = 1
LANES = 128
MESH = pl.DeviceIdType.MESH


def kernel(cfg, d_hbm, g_hbm, x_ref, dv, gv, t1, t2, r1f, r2f, rb, acc,
           msg, gath, zmsg, zgath,
           load_sem, ring_send, ring_recv, pl_send, pl_recv, z_send, z_recv):
    n_p, n_z, rows, sh, cuts, rows_all = cfg
    me_p = lax.axis_index("param")
    me_z = lax.axis_index("walker")
    groups = sh // 8

    def base(k):
        return pl.multiple_of(lax.rem(me_z + (k + n_z), n_z) * sh, 8)

    barrier = pltpu.get_barrier_semaphore()

    def greet_p(i, c):
        pl.semaphore_signal(barrier, inc=1, device_id={"param": lax.rem(me_p + i, n_p)}, device_id_type=MESH)
        return c

    def greet_z(i, c):
        pl.semaphore_signal(barrier, inc=1, device_id={"walker": lax.rem(me_z + i, n_z)}, device_id_type=MESH)
        return c

    pltpu.make_async_copy(g_hbm, gv, load_sem.at[n_z]).start()
    for k in range(n_z):
        if k == 1:
            lax.fori_loop(1, n_p, greet_p, 0)
            lax.fori_loop(1, n_z, greet_z, 0)
        at = pl.ds(k * sh, sh)
        for r in range(rows):
            pltpu.make_async_copy(d_hbm.at[at, r, :], dv.at[r, at, :], load_sem.at[k]).start()

    def loaded(k):
        part = dv.at[:, pl.ds(pl.multiple_of(k * sh, 8), sh), :]
        pltpu.make_async_copy(part, part, load_sem.at[k]).wait()

    def accum(vec, others, ready=None):
        n = rows + 1 + len(others)

        def shard(k, a):
            if ready is not None:
                ready(k)
            out = list(a)
            for i in range(groups):
                o = pl.multiple_of(k * sh + i * 8, 8)
                v = vec[pl.ds(o, 8), :]
                for r in range(rows):
                    out[r] = out[r] + dv[r, pl.ds(o, 8), :] * v
                out[rows] = out[rows] + v * v
                for j, ref in enumerate(others):
                    out[rows + 1 + j] = out[rows + 1 + j] + ref[pl.ds(o, 8), :] * v
            return tuple(out)

        a = lax.fori_loop(0, n_z, shard, tuple(jnp.zeros((8, LANES), jnp.float32) for _ in range(n)))
        for i in range(n):
            acc[i] = a[i]

    sub = lax.broadcasted_iota(jnp.int32, (16, LANES), 0)
    lane = lax.broadcasted_iota(jnp.int32, (16, LANES), 1)
    diag = sub == lane

    def plane_sum(it):
        part = jnp.sum(acc[...], axis=1)
        part = jnp.sum(part, axis=1, keepdims=True)
        row = jnp.sum(jnp.where(diag, part, 0.0), axis=0, keepdims=True)
        msg[it] = row
        gath[it, me_p] = row
        if it == 0:
            pl.semaphore_wait(barrier, n_p - 1 + n_z - 1)

        def send(i, c):
            peer = lax.rem(me_p + i, n_p)
            pltpu.make_async_remote_copy(msg.at[it], gath.at[it, me_p], pl_send.at[it], pl_recv.at[it],
                                         device_id={"param": peer}, device_id_type=MESH).start()
            return c

        lax.fori_loop(1, n_p, send, 0)
        every = gath.at[it, pl.ds(0, n_p - 1)]
        pltpu.make_async_copy(every, every, pl_recv.at[it]).wait()
        tot = jnp.sum(gath[it, :, 0, :], axis=0, keepdims=True)
        tot = jnp.sum(jnp.where(diag, tot, 0.0), axis=1, keepdims=True)
        return jnp.broadcast_to(tot, (16, LANES))

    def z_start(it, w):
        row = jnp.sum(w * w, axis=0, keepdims=True)
        zmsg[it] = row
        zgath[it, me_z] = row

        def send(i, c):
            peer = lax.rem(me_z + i, n_z)
            pltpu.make_async_remote_copy(zmsg.at[it], zgath.at[it, me_z], z_send.at[it], z_recv.at[it],
                                         device_id={"walker": peer}, device_id_type=MESH).start()
            return c

        lax.fori_loop(1, n_z, send, 0)

    def z_finish(it):
        every = zgath.at[it, pl.ds(0, n_z - 1)]
        pltpu.make_async_copy(every, every, z_recv.at[it]).wait()
        return jnp.sum(zgath[it, :, 0, :], axis=0, keepdims=True)

    def project(first, count, t, wv):
        def shard(k, c):
            b = base(first + k)
            for i in range(groups):
                o = pl.multiple_of(b + i * 8, 8)
                s = dv[0, pl.ds(o, 8), :] * wv[0]
                for r in range(1, rows):
                    s = s + dv[r, pl.ds(o, 8), :] * wv[r]
                t[pl.ds(o, 8), :] = s
            return c

        lax.fori_loop(0, count, shard, 0)

    pieces = tuple((cuts[c], cuts[c + 1] - cuts[c]) for c in range(len(cuts) - 1))
    n_c = len(pieces)
    far = (range(n_c // 2), range(n_c // 2, n_c))
    signs = (1, -1)

    def ring(it, phase, way, kind, c, hops, src, dst):
        return pltpu.make_async_remote_copy(
            src, dst, ring_send.at[it, phase], ring_recv.at[it, phase, way, kind, c],
            device_id={"walker": lax.rem(me_z + n_z + signs[way] * hops, n_z)}, device_id_type=MESH)

    def span(k, c):
        lo, n = pieces[c]
        return pl.ds(pl.multiple_of(base(k) + lo, 8), n)

    def reduce_scatter(it, t, w, meanwhile, finish):
        wv = [jnp.broadcast_to(w[r:r + 1, :], (8, LANES)) for r in range(rows)]

        def copy(way, kind, c, k, hops):
            lo, n = pieces[c]
            return ring(it, 0, way, kind, c, hops, t.at[span(signs[way] * k, c), :],
                        rb.at[it, way, kind, pl.ds(lo, n), :])

        def landed(way, kind, c):
            lo, n = pieces[c]
            return rb[it, way, kind, pl.ds(lo, n), :]

        project(3, 3, t, wv)
        for c in range(n_c):
            for way in range(2):
                if c in far[way]:
                    copy(way, 0, c, 4, 2).start()
            for way in range(2):
                copy(way, 1, c, 3, 1).start()
        project(6, 5, t, wv)
        meanwhile()

        def direct(c):
            for way in range(2):
                copy(way, 2, c, 1, 1).start()

        for c in range(AHEAD):
            direct(c)
        for c in range(n_c):
            for way in range(2):
                copy(way, 1, c, 3, 1).wait_recv()
                s = landed(way, 1, c)
                if c in far[way]:
                    copy(way, 0, c, 4, 2).wait_recv()
                    s = s + landed(way, 0, c)
                t[span(signs[way] * 2, c), :] += s
                copy(way, 3, c, 2, 2).start()
            if c + AHEAD < n_c:
                direct(c + AHEAD)
        scale = finish(None)
        for c in range(n_c):
            s = t[span(0, c), :]
            for way in range(2):
                copy(way, 2, c, 1, 1).wait_recv()
                copy(way, 3, c, 2, 2).wait_recv()
                s = s + (landed(way, 2, c) + landed(way, 3, c))
            t[span(0, c), :] = s
            finish(c, s, scale)

    def gather_copy(it, rf, way, kind, c, k, hops):
        piece = rf.at[span(-signs[way] * k, c), :]
        return ring(it, 1, way, kind, c, hops, piece, piece)

    def gather_start(it, rf, c):
        for way in range(2):
            gather_copy(it, rf, way, 0, c, 0, 2).start()

    def gather_near(it, rf, c):
        for way in range(2):
            gather_copy(it, rf, way, 1, c, 0, 1).start()

    def gather_finish(it, rf):
        for c in range(n_c // 2):
            gather_near(it, rf, c)
        for c in range(n_c):
            for way in range(2):
                gather_copy(it, rf, way, 0, c, 0, 2).wait_recv()
                if c in far[way]:
                    gather_copy(it, rf, way, 3, c, 2, 2).start()
                gather_copy(it, rf, way, 2, c, 2, 1).start()
            if c >= n_c // 2:
                gather_near(it, rf, c)
        for c in range(n_c):
            for way in range(2):
                gather_copy(it, rf, way, 1, c, 0, 1).wait_recv()
                gather_copy(it, rf, way, 2, c, 2, 1).wait_recv()
                if c in far[way]:
                    gather_copy(it, rf, way, 3, c, 2, 2).wait_recv()

    own = pl.ds(base(0), sh)
    inv = 1.0 / rows_all

    acc[...] = jnp.zeros_like(acc)
    pltpu.make_async_copy(g_hbm, gv, load_sem.at[n_z]).wait()
    accum(gv, (), loaded)
    tot = plane_sum(0)
    w0, rr0 = tot[:rows], tot[rows:rows + 1]
    pp0 = rr0
    a0 = []

    def residual1(c, s=None, a=None):
        if c is None:
            a0.append(rr0 / (z_finish(0) * inv + DAMPING * pp0))
            return a0[0]
        at = span(0, c)
        r1f[at, :] = gv[at, :] - a * (s * inv + DAMPING * gv[at, :])
        gather_start(0, r1f, c)

    reduce_scatter(0, t1, w0, lambda: z_start(0, w0), residual1)
    gather_finish(0, r1f)
    accum(r1f, (gv,))

    tot = plane_sum(1)
    rr1, rp1 = tot[rows:rows + 1], tot[rows + 1:rows + 2]
    b0 = rr1 / rr0
    u1 = tot[:rows]
    w1 = u1 + b0 * w0
    pp1 = rr1 + b0 * (2.0 * rp1 + b0 * pp0)
    a1 = []

    def residual2(c, s=None, a=None):
        if c is None:
            a1.append(rr1 / (z_finish(1) * inv + DAMPING * pp1))
            return a1[0]
        at = span(0, c)
        p1 = r1f[at, :] + b0 * gv[at, :]
        r2f[at, :] = r1f[at, :] - a * ((s + b0 * t1[at, :]) * inv + DAMPING * p1)
        gather_start(1, r2f, c)

    reduce_scatter(1, t2, u1, lambda: z_start(1, w1), residual2)
    gather_finish(1, r2f)
    accum(r2f, (gv, r1f))

    tot = plane_sum(2)
    rr2, rg2, rq2 = tot[rows:rows + 1], tot[rows + 1:rows + 2], tot[rows + 2:rows + 3]
    b1 = rr2 / rr1
    w2 = tot[:rows] + b1 * w1
    pp2 = rr2 + b1 * (2.0 * (rq2 + b0 * rg2) + b1 * pp1)
    z_start(2, w2)
    p1 = r1f[own, :] + b0 * gv[own, :]
    x1 = a0[0] * gv[own, :] + a1[0] * p1
    p2 = r2f[own, :] + b1 * p1
    a2 = rr2 / (z_finish(2) * inv + DAMPING * pp2)
    x_ref[...] = x1 + a2 * p2

    sent = pl.ds(0, (n_z - 1) * sh)
    for it in range(2):
        for phase, ref in enumerate(((t1, t2)[it], (r1f, r2f)[it])):
            every = ref.at[sent, :]
            pltpu.make_async_copy(every, every, ring_send.at[it, phase]).wait()
    for it in range(3):
        every = gath.at[it, pl.ds(0, n_p - 1)]
        pltpu.make_async_copy(every, every, pl_send.at[it]).wait()
        every = zgath.at[it, pl.ds(0, n_z - 1)]
        pltpu.make_async_copy(every, every, z_send.at[it]).wait()


def body(derivs, gradient):
    n_p, n_z = lax.axis_size("param"), lax.axis_size("walker")
    rows, cols = derivs.shape
    tiles = cols // LANES
    sh = tiles // n_z
    cuts = tuple((sh // 8 * c + PIECES - 1) // PIECES * 8 for c in range(PIECES + 1))
    d = derivs.reshape(rows, tiles, LANES).transpose(1, 0, 2)
    g = gradient.reshape(tiles, LANES)
    f32 = jnp.float32
    full = pltpu.VMEM((tiles, LANES), f32)
    x = pl.pallas_call(
        functools.partial(kernel, (n_p, n_z, rows, sh, cuts, rows * n_z)),
        out_shape=jax.ShapeDtypeStruct((sh, LANES), f32),
        in_specs=[pl.BlockSpec(memory_space=pltpu.HBM)] * 2,
        out_specs=pl.BlockSpec(memory_space=pltpu.VMEM),
        scratch_shapes=[
            pltpu.VMEM((rows, tiles, LANES), f32),
            full, full, full, full, full,
            pltpu.VMEM((2, 2, 4, sh, LANES), f32),
            pltpu.VMEM((16, 8, LANES), f32),
            pltpu.VMEM((3, 1, LANES), f32),
            pltpu.VMEM((3, n_p, 1, LANES), f32),
            pltpu.VMEM((3, 1, LANES), f32),
            pltpu.VMEM((3, n_z, 1, LANES), f32),
            pltpu.SemaphoreType.DMA((n_z + 1,)),
            pltpu.SemaphoreType.DMA((2, 2)),
            pltpu.SemaphoreType.DMA((2, 2, 2, 4, PIECES)),
            pltpu.SemaphoreType.DMA((3,)),
            pltpu.SemaphoreType.DMA((3,)),
            pltpu.SemaphoreType.DMA((3,)),
            pltpu.SemaphoreType.DMA((3,)),
        ],
        compiler_params=pltpu.CompilerParams(
            collective_id=0, has_side_effects=True, vmem_limit_bytes=56 * 1024 * 1024),
        name="cg_solve",
    )(d, g)
    return x.reshape(sh * LANES)


def solution(mesh):
    in_specs = (P("walker", "param"), P("param"))
    out_specs = P(("param", "walker"))
    return jax.shard_map(body, mesh=mesh, in_specs=in_specs, out_specs=out_specs, check_vma=False)
```

```python
import functools
import itertools

import jax
import jax.numpy as jnp
from jax import lax
from jax.experimental import pallas as pl
from jax.experimental.pallas import tpu as pltpu
from jax.sharding import PartitionSpec as P

DAMPING = 0.001
PIECES = 4
ROUTES = (
    (0, 0, 0, 4, 3), (0, 0, 1, 3, 2), (0, 0, 0, 2, 1), (0, 1, 1, 4, 3), (0, 1, 0, 3, 2), (0, 1, 1, 2, 1),
    (0, 2, 0, 4, 3), (0, 2, 1, 3, 2), (0, 2, 0, 2, 1), (0, 3, 1, 4, 3), (0, 3, 0, 3, 2), (0, 3, 1, 2, 1),
    (0, 0, 1, 1, 0), (0, 1, 0, 1, 0), (0, 2, 1, 1, 0), (0, 3, 0, 1, 0), (0, 0, 0, 3, 0), (0, 0, 1, 2, 0),
    (0, 0, 0, 1, 0), (0, 1, 1, 3, 0), (0, 1, 0, 2, 0), (0, 1, 1, 1, 0), (0, 2, 0, 3, 0), (0, 2, 1, 2, 0),
    (0, 3, 1, 3, 0), (0, 2, 0, 1, 0), (0, 3, 1, 1, 0), (0, 3, 0, 2, 0), (1, 0, 0, 0, 2), (1, 0, 0, 0, 1),
    (1, 0, 1, 0, 2), (1, 0, 1, 0, 1), (1, 1, 0, 0, 2), (1, 1, 1, 0, 2), (1, 2, 0, 0, 2), (1, 2, 1, 0, 2),
    (1, 3, 0, 0, 2), (1, 3, 1, 0, 2), (1, 0, 0, 2, 4), (1, 0, 0, 2, 3), (1, 0, 1, 2, 3), (1, 1, 0, 0, 1),
    (1, 1, 1, 0, 1), (1, 1, 0, 2, 3), (1, 1, 1, 2, 4), (1, 1, 1, 2, 3), (1, 2, 0, 0, 1), (1, 2, 1, 0, 1),
    (1, 2, 0, 2, 4), (1, 2, 0, 2, 3), (1, 2, 1, 2, 3), (1, 3, 0, 0, 1), (1, 3, 1, 0, 1), (1, 3, 0, 2, 3),
    (1, 3, 1, 2, 4), (1, 3, 1, 2, 3),
)
LANES = 128
MESH = pl.DeviceIdType.MESH


def kernel(cfg, d_hbm, g_hbm, x_ref, dv, gv, t1, t2, r1f, r2f, rb, acc,
           msg, gath, zmsg, zgath,
           load_sem, ring_send, ring_recv, pl_send, pl_recv, z_send, z_recv):
    n_p, n_z, rows, sh, cuts, rows_all = cfg
    me_p = lax.axis_index("param")
    me_z = lax.axis_index("walker")
    groups = sh // 8

    def base(k):
        return pl.multiple_of(lax.rem(me_z + (k + n_z), n_z) * sh, 8)

    y, x, core = me_p // 8, lax.rem(me_p // 2, 4), lax.rem(me_p, 2)
    ys, xs, cores = ([lax.rem(at + i, n) for i in range(n)] for at, n in ((y, 4), (x, 4), (core, 2)))
    plane = [(ys[j] * 4 + xs[i]) * 2 + cores[k]
             for j, i, k in sorted(itertools.product(range(4), range(4), range(2)),
                                   key=lambda s: -min(s[0], 4 - s[0]) - min(s[1], 4 - s[1]) - 0.1 * s[2])
             if (j, i, k) != (0, 0, 0)]

    barrier = pltpu.get_barrier_semaphore()

    def greet_z(i, c):
        pl.semaphore_signal(barrier, inc=1, device_id={"walker": lax.rem(me_z + i, n_z)}, device_id_type=MESH)
        return c

    pltpu.make_async_copy(g_hbm, gv, load_sem.at[n_z]).start()
    for k in range(n_z):
        if k == 1:
            for peer in plane:
                pl.semaphore_signal(barrier, inc=1, device_id={"param": peer}, device_id_type=MESH)
            lax.fori_loop(1, n_z, greet_z, 0)
        at = pl.ds(k * sh, sh)
        for r in range(rows):
            pltpu.make_async_copy(d_hbm.at[at, r, :], dv.at[r, at, :], load_sem.at[k]).start()

    def loaded(k):
        part = dv.at[:, pl.ds(pl.multiple_of(k * sh, 8), sh), :]
        pltpu.make_async_copy(part, part, load_sem.at[k]).wait()

    def accum(vec, others, ready=None, first=0, count=None, more=False):
        n = rows + 1 + len(others)

        def shard(k, a):
            if ready is not None:
                ready(k)
            b = k * sh if first is None else pl.multiple_of(lax.rem(me_z + (first + k), n_z) * sh, 8)
            out = list(a)
            for i in range(groups):
                o = pl.multiple_of(b + i * 8, 8)
                v = vec[pl.ds(o, 8), :]
                for r in range(rows):
                    out[r] = out[r] + dv[r, pl.ds(o, 8), :] * v
                out[rows] = out[rows] + v * v
                for j, ref in enumerate(others):
                    out[rows + 1 + j] = out[rows + 1 + j] + ref[pl.ds(o, 8), :] * v
            return tuple(out)

        init = tuple(acc[i] if more else jnp.zeros((8, LANES), jnp.float32) for i in range(n))
        a = lax.fori_loop(0, n_z if count is None else count, shard, init)
        for i in range(n):
            acc[i] = a[i]

    sub = lax.broadcasted_iota(jnp.int32, (16, LANES), 0)
    lane = lax.broadcasted_iota(jnp.int32, (16, LANES), 1)
    diag = sub == lane

    def plane_sum(it):
        part = jnp.sum(acc[...], axis=1)
        part = jnp.sum(part, axis=1, keepdims=True)
        row = jnp.sum(jnp.where(diag, part, 0.0), axis=0, keepdims=True)
        msg[it] = row
        gath[it, me_p] = row
        if it == 0:
            pl.semaphore_wait(barrier, n_p - 1 + n_z - 1)

        for peer in plane:
            pltpu.make_async_remote_copy(msg.at[it], gath.at[it, me_p], pl_send.at[it], pl_recv.at[it],
                                         device_id={"param": peer}, device_id_type=MESH).start()
        every = gath.at[it, pl.ds(0, n_p - 1)]
        pltpu.make_async_copy(every, every, pl_recv.at[it]).wait()
        tot = jnp.sum(gath[it, :, 0, :], axis=0, keepdims=True)
        tot = jnp.sum(jnp.where(diag, tot, 0.0), axis=1, keepdims=True)
        return jnp.broadcast_to(tot, (16, LANES))

    def z_start(it, w):
        row = jnp.sum(w * w, axis=0, keepdims=True)
        zmsg[it] = row
        zgath[it, me_z] = row

        def send(i, c):
            peer = lax.rem(me_z + i, n_z)
            pltpu.make_async_remote_copy(zmsg.at[it], zgath.at[it, me_z], z_send.at[it], z_recv.at[it],
                                         device_id={"walker": peer}, device_id_type=MESH).start()
            return c

        lax.fori_loop(1, n_z, send, 0)

    def z_finish(it):
        every = zgath.at[it, pl.ds(0, n_z - 1)]
        pltpu.make_async_copy(every, every, z_recv.at[it]).wait()
        return jnp.sum(zgath[it, :, 0, :], axis=0, keepdims=True)

    def project(first, count, t, wv):
        def shard(k, c):
            b = base(first + k)
            for i in range(groups):
                o = pl.multiple_of(b + i * 8, 8)
                s = dv[0, pl.ds(o, 8), :] * wv[0]
                for r in range(1, rows):
                    s = s + dv[r, pl.ds(o, 8), :] * wv[r]
                t[pl.ds(o, 8), :] = s
            return c

        lax.fori_loop(0, count, shard, 0)

    pieces = tuple((cuts[c], cuts[c + 1] - cuts[c]) for c in range(len(cuts) - 1))
    signs = (1, -1)

    def span(k, c):
        lo, n = pieces[c]
        return pl.ds(pl.multiple_of(base(k) + lo, 8), n)

    def exchange(it, t, w, rf, others, meanwhile, finish):
        wv = [jnp.broadcast_to(w[r:r + 1, :], (8, LANES)) for r in range(rows)]

        def copy(phase, c, way, a, b):
            lo, n = pieces[c]
            sign = signs[way]
            if phase == 0:
                src, dst = t.at[span(sign * a, c), :], rb.at[it, way, a - 1, pl.ds(lo, n), :]
                slot = a - 1
            else:
                src = dst = rf.at[span(-sign * a, c), :]
                slot = b - 1
            peer = lax.rem(me_z + (n_z + sign * abs(a - b)), n_z)
            return pltpu.make_async_remote_copy(
                src, dst, ring_send.at[it, phase], ring_recv.at[it, phase, way, slot, c],
                device_id={"walker": peer}, device_id_type=MESH)

        def arrive(phase, c, way, at):
            total = None
            for route in ROUTES:
                if route[:3] == (phase, c, way) and route[4] == at and route not in waited:
                    waited.add(route)
                    copy(*route).wait_recv()
                    if phase == 0:
                        lo, n = pieces[c]
                        part = rb[it, way, route[3] - 1, pl.ds(lo, n), :]
                        total = part if total is None else total + part
            return total

        waited, done = set(), set()
        project(3, 3, t, wv)
        for phase, c, way, a, b in ROUTES:
            if phase == 0:
                if a < 3 and "rest" not in done:
                    project(6, 5, t, wv)
                    done.add("rest")
                s = arrive(0, c, way, a)
                if s is not None:
                    t[span(signs[way] * a, c), :] += s
            elif a == 0:
                if c not in done:
                    if "scale" not in done:
                        finish(None, None)
                        done.add("scale")
                    s = t[span(0, c), :]
                    for w_ in range(2):
                        s = s + arrive(0, c, w_, 0)
                    t[span(0, c), :] = s
                    finish(c, s)
                    done.add(c)
            else:
                arrive(1, c, way, a)
            copy(phase, c, way, a, b).start()
            if "z" not in done and "rest" in done:
                meanwhile()
                done.add("z")
        for far in (False, True):
            for route in ROUTES:
                if route[0] == 1 and (route[4] > 2) == far:
                    arrive(1, route[1], route[2], route[4])
            if far:
                accum(rf, others, None, 3, 3, True)
            else:
                accum(rf, others, None, 6, 5)

    own = pl.ds(base(0), sh)
    inv = 1.0 / rows_all

    acc[...] = jnp.zeros_like(acc)
    pltpu.make_async_copy(g_hbm, gv, load_sem.at[n_z]).wait()
    accum(gv, (), loaded, None)
    tot = plane_sum(0)
    w0, rr0 = tot[:rows], tot[rows:rows + 1]
    pp0 = rr0
    a0 = []

    def residual1(c, s):
        if c is None:
            a0.append(rr0 / (z_finish(0) * inv + DAMPING * pp0))
            return
        at = span(0, c)
        r1f[at, :] = gv[at, :] - a0[0] * (s * inv + DAMPING * gv[at, :])

    exchange(0, t1, w0, r1f, (gv,), lambda: z_start(0, w0), residual1)

    tot = plane_sum(1)
    rr1, rp1 = tot[rows:rows + 1], tot[rows + 1:rows + 2]
    b0 = rr1 / rr0
    u1 = tot[:rows]
    w1 = u1 + b0 * w0
    pp1 = rr1 + b0 * (2.0 * rp1 + b0 * pp0)
    a1 = []

    def residual2(c, s):
        if c is None:
            a1.append(rr1 / (z_finish(1) * inv + DAMPING * pp1))
            return
        at = span(0, c)
        p1 = r1f[at, :] + b0 * gv[at, :]
        r2f[at, :] = r1f[at, :] - a1[0] * ((s + b0 * t1[at, :]) * inv + DAMPING * p1)

    exchange(1, t2, u1, r2f, (gv, r1f), lambda: z_start(1, w1), residual2)

    tot = plane_sum(2)
    rr2, rg2, rq2 = tot[rows:rows + 1], tot[rows + 1:rows + 2], tot[rows + 2:rows + 3]
    b1 = rr2 / rr1
    w2 = tot[:rows] + b1 * w1
    pp2 = rr2 + b1 * (2.0 * (rq2 + b0 * rg2) + b1 * pp1)
    z_start(2, w2)
    p1 = r1f[own, :] + b0 * gv[own, :]
    x1 = a0[0] * gv[own, :] + a1[0] * p1
    p2 = r2f[own, :] + b1 * p1
    a2 = rr2 / (z_finish(2) * inv + DAMPING * pp2)
    x_ref[...] = x1 + a2 * p2

    sent = pl.ds(0, (n_z - 1) * sh)
    for it in range(2):
        for phase, ref in enumerate(((t1, t2)[it], (r1f, r2f)[it])):
            every = ref.at[sent, :]
            pltpu.make_async_copy(every, every, ring_send.at[it, phase]).wait()
    for it in range(3):
        every = gath.at[it, pl.ds(0, n_p - 1)]
        pltpu.make_async_copy(every, every, pl_send.at[it]).wait()
        every = zgath.at[it, pl.ds(0, n_z - 1)]
        pltpu.make_async_copy(every, every, z_send.at[it]).wait()


def body(derivs, gradient):
    n_p, n_z = lax.axis_size("param"), lax.axis_size("walker")
    rows, cols = derivs.shape
    tiles = cols // LANES
    sh = tiles // n_z
    cuts = tuple((sh // 8 * c + PIECES - 1) // PIECES * 8 for c in range(PIECES + 1))
    d = derivs.reshape(rows, tiles, LANES).transpose(1, 0, 2)
    g = gradient.reshape(tiles, LANES)
    f32 = jnp.float32
    full = pltpu.VMEM((tiles, LANES), f32)
    x = pl.pallas_call(
        functools.partial(kernel, (n_p, n_z, rows, sh, cuts, rows * n_z)),
        out_shape=jax.ShapeDtypeStruct((sh, LANES), f32),
        in_specs=[pl.BlockSpec(memory_space=pltpu.HBM)] * 2,
        out_specs=pl.BlockSpec(memory_space=pltpu.VMEM),
        scratch_shapes=[
            pltpu.VMEM((rows, tiles, LANES), f32),
            full, full, full, full, full,
            pltpu.VMEM((2, 2, 4, sh, LANES), f32),
            pltpu.VMEM((16, 8, LANES), f32),
            pltpu.VMEM((3, 1, LANES), f32),
            pltpu.VMEM((3, n_p, 1, LANES), f32),
            pltpu.VMEM((3, 1, LANES), f32),
            pltpu.VMEM((3, n_z, 1, LANES), f32),
            pltpu.SemaphoreType.DMA((n_z + 1,)),
            pltpu.SemaphoreType.DMA((2, 2)),
            pltpu.SemaphoreType.DMA((2, 2, 2, 4, PIECES)),
            pltpu.SemaphoreType.DMA((3,)),
            pltpu.SemaphoreType.DMA((3,)),
            pltpu.SemaphoreType.DMA((3,)),
            pltpu.SemaphoreType.DMA((3,)),
        ],
        compiler_params=pltpu.CompilerParams(
            collective_id=0, has_side_effects=True, vmem_limit_bytes=56 * 1024 * 1024),
        name="cg_solve",
    )(d, g)
    return x.reshape(sh * LANES)


def solution(mesh):
    in_specs = (P("walker", "param"), P("param"))
    out_specs = P(("param", "walker"))
    return jax.shard_map(body, mesh=mesh, in_specs=in_specs, out_specs=out_specs, check_vma=False)
```

```python
import functools
import itertools

import jax
import jax.numpy as jnp
from jax import lax
from jax.experimental import pallas as pl
from jax.experimental.pallas import tpu as pltpu
from jax.sharding import PartitionSpec as P

DAMPING = 0.001
PIECES = 4
ROUTES = (
    (0, 0, 0, 4, 3), (0, 0, 1, 3, 2), (0, 0, 0, 2, 1), (0, 1, 1, 4, 3), (0, 1, 0, 3, 2), (0, 1, 1, 2, 1),
    (0, 2, 0, 4, 3), (0, 2, 1, 3, 2), (0, 2, 0, 2, 1), (0, 3, 1, 4, 3), (0, 3, 0, 3, 2), (0, 3, 1, 2, 1),
    (0, 0, 1, 1, 0), (0, 1, 0, 1, 0), (0, 0, 0, 3, 0), (0, 0, 1, 2, 0), (0, 0, 0, 1, 0), (0, 1, 1, 3, 0),
    (0, 1, 0, 2, 0), (0, 1, 1, 1, 0), (0, 2, 0, 3, 0), (0, 2, 1, 2, 0), (0, 2, 1, 1, 0), (0, 3, 1, 3, 0),
    (0, 2, 0, 1, 0), (0, 3, 1, 1, 0), (0, 3, 0, 2, 0), (0, 3, 0, 1, 0), (1, 0, 0, 0, 2), (1, 0, 0, 0, 1),
    (1, 0, 1, 0, 2), (1, 0, 1, 0, 1), (1, 1, 0, 0, 2), (1, 1, 1, 0, 2), (1, 2, 0, 0, 2), (1, 2, 1, 0, 2),
    (1, 3, 0, 0, 2), (1, 3, 1, 0, 2), (1, 0, 0, 2, 4), (1, 0, 0, 2, 3), (1, 0, 1, 2, 3), (1, 1, 0, 0, 1),
    (1, 1, 1, 0, 1), (1, 1, 0, 2, 3), (1, 1, 1, 2, 4), (1, 1, 1, 2, 3), (1, 2, 0, 0, 1), (1, 2, 1, 0, 1),
    (1, 2, 0, 2, 4), (1, 2, 0, 2, 3), (1, 2, 1, 2, 3), (1, 3, 0, 0, 1), (1, 3, 1, 0, 1), (1, 3, 0, 2, 3),
    (1, 3, 1, 2, 4), (1, 3, 1, 2, 3),
)
LANES = 128
MESH = pl.DeviceIdType.MESH


def kernel(cfg, d_hbm, g_hbm, x_ref, dv, gv, t1, t2, r1f, r2f, rb, acc,
           msg, gath, zmsg, zgath,
           load_sem, ring_send, ring_recv, pl_send, pl_recv, z_send, z_recv):
    n_p, n_z, rows, sh, cuts, rows_all = cfg
    me_p = lax.axis_index("param")
    me_z = lax.axis_index("walker")
    groups = sh // 8

    def base(k):
        return pl.multiple_of(lax.rem(me_z + (k + n_z), n_z) * sh, 8)

    y, x, core = me_p // 8, lax.rem(me_p // 2, 4), lax.rem(me_p, 2)
    ys, xs, cores = ([lax.rem(at + i, n) for i in range(n)] for at, n in ((y, 4), (x, 4), (core, 2)))
    plane = [(ys[j] * 4 + xs[i]) * 2 + cores[k]
             for j, i, k in sorted(itertools.product(range(4), range(4), range(2)),
                                   key=lambda s: -min(s[0], 4 - s[0]) - min(s[1], 4 - s[1]) - 0.1 * s[2])
             if (j, i, k) != (0, 0, 0)]

    barrier = pltpu.get_barrier_semaphore()

    def greet_z(i, c):
        pl.semaphore_signal(barrier, inc=1, device_id={"walker": lax.rem(me_z + i, n_z)}, device_id_type=MESH)
        return c

    pltpu.make_async_copy(g_hbm, gv, load_sem.at[n_z]).start()
    for k in range(n_z):
        if k == 1:
            for peer in plane:
                pl.semaphore_signal(barrier, inc=1, device_id={"param": peer}, device_id_type=MESH)
            lax.fori_loop(1, n_z, greet_z, 0)
        at = pl.ds(k * sh, sh)
        for r in range(rows):
            pltpu.make_async_copy(d_hbm.at[at, r, :], dv.at[r, at, :], load_sem.at[k]).start()

    def loaded(k):
        part = dv.at[:, pl.ds(pl.multiple_of(k * sh, 8), sh), :]
        pltpu.make_async_copy(part, part, load_sem.at[k]).wait()

    def accum(vec, others, ready=None, first=0, count=None, more=False):
        n = rows + 1 + len(others)

        def shard(k, a):
            if ready is not None:
                ready(k)
            b = k * sh if first is None else pl.multiple_of(lax.rem(me_z + (first + k), n_z) * sh, 8)
            out = list(a)
            for i in range(groups):
                o = pl.multiple_of(b + i * 8, 8)
                v = vec[pl.ds(o, 8), :]
                for r in range(rows):
                    out[r] = out[r] + dv[r, pl.ds(o, 8), :] * v
                out[rows] = out[rows] + v * v
                for j, ref in enumerate(others):
                    out[rows + 1 + j] = out[rows + 1 + j] + ref[pl.ds(o, 8), :] * v
            return tuple(out)

        init = tuple(acc[i] if more else jnp.zeros((8, LANES), jnp.float32) for i in range(n))
        a = lax.fori_loop(0, n_z if count is None else count, shard, init)
        for i in range(n):
            acc[i] = a[i]

    sub = lax.broadcasted_iota(jnp.int32, (16, LANES), 0)
    lane = lax.broadcasted_iota(jnp.int32, (16, LANES), 1)
    diag = sub == lane

    def plane_sum(it):
        part = jnp.sum(acc[...], axis=1)
        part = jnp.sum(part, axis=1, keepdims=True)
        row = jnp.sum(jnp.where(diag, part, 0.0), axis=0, keepdims=True)
        msg[it] = row
        gath[it, me_p] = row
        if it == 0:
            pl.semaphore_wait(barrier, n_p - 1 + n_z - 1)

        for peer in plane:
            pltpu.make_async_remote_copy(msg.at[it], gath.at[it, me_p], pl_send.at[it], pl_recv.at[it],
                                         device_id={"param": peer}, device_id_type=MESH).start()
        every = gath.at[it, pl.ds(0, n_p - 1)]
        pltpu.make_async_copy(every, every, pl_recv.at[it]).wait()
        tot = jnp.sum(gath[it, :, 0, :], axis=0, keepdims=True)
        tot = jnp.sum(jnp.where(diag, tot, 0.0), axis=1, keepdims=True)
        return jnp.broadcast_to(tot, (16, LANES))

    def z_start(it, w):
        row = jnp.sum(w * w, axis=0, keepdims=True)
        zmsg[it] = row
        zgath[it, me_z] = row

        def send(i, c):
            peer = lax.rem(me_z + i, n_z)
            pltpu.make_async_remote_copy(zmsg.at[it], zgath.at[it, me_z], z_send.at[it], z_recv.at[it],
                                         device_id={"walker": peer}, device_id_type=MESH).start()
            return c

        lax.fori_loop(1, n_z, send, 0)

    def z_finish(it):
        every = zgath.at[it, pl.ds(0, n_z - 1)]
        pltpu.make_async_copy(every, every, z_recv.at[it]).wait()
        return jnp.sum(zgath[it, :, 0, :], axis=0, keepdims=True)

    def project(first, count, t, wv):
        def shard(k, c):
            b = base(first + k)
            for i in range(groups):
                o = pl.multiple_of(b + i * 8, 8)
                s = dv[0, pl.ds(o, 8), :] * wv[0]
                for r in range(1, rows):
                    s = s + dv[r, pl.ds(o, 8), :] * wv[r]
                t[pl.ds(o, 8), :] = s
            return c

        lax.fori_loop(0, count, shard, 0)

    pieces = tuple((cuts[c], cuts[c + 1] - cuts[c]) for c in range(len(cuts) - 1))
    signs = (1, -1)

    def span(k, c):
        lo, n = pieces[c]
        return pl.ds(pl.multiple_of(base(k) + lo, 8), n)

    def exchange(it, t, w, rf, others, meanwhile, finish):
        wv = [jnp.broadcast_to(w[r:r + 1, :], (8, LANES)) for r in range(rows)]

        def copy(phase, c, way, a, b):
            lo, n = pieces[c]
            sign = signs[way]
            if phase == 0:
                src, dst = t.at[span(sign * a, c), :], rb.at[it, way, a - 1, pl.ds(lo, n), :]
                slot = a - 1
            else:
                src = dst = rf.at[span(-sign * a, c), :]
                slot = b - 1
            peer = lax.rem(me_z + (n_z + sign * abs(a - b)), n_z)
            return pltpu.make_async_remote_copy(
                src, dst, ring_send.at[it, phase], ring_recv.at[it, phase, way, slot, c],
                device_id={"walker": peer}, device_id_type=MESH)

        def arrive(phase, c, way, at):
            total = None
            for route in ROUTES:
                if route[:3] == (phase, c, way) and route[4] == at and route not in waited:
                    waited.add(route)
                    copy(*route).wait_recv()
                    if phase == 0:
                        lo, n = pieces[c]
                        part = rb[it, way, route[3] - 1, pl.ds(lo, n), :]
                        total = part if total is None else total + part
            return total

        waited, done = set(), set()
        project(3, 3, t, wv)
        for phase, c, way, a, b in ROUTES:
            if phase == 0:
                if a < 3 and "rest" not in done:
                    project(6, 5, t, wv)
                    done.add("rest")
                s = arrive(0, c, way, a)
                if s is not None:
                    t[span(signs[way] * a, c), :] += s
            elif a == 0:
                if c not in done:
                    if "scale" not in done:
                        finish(None, None)
                        done.add("scale")
                    s = t[span(0, c), :]
                    for w_ in range(2):
                        s = s + arrive(0, c, w_, 0)
                    t[span(0, c), :] = s
                    finish(c, s)
                    done.add(c)
            else:
                arrive(1, c, way, a)
            copy(phase, c, way, a, b).start()
            if "z" not in done and "rest" in done:
                meanwhile()
                done.add("z")
        for far in (False, True):
            for route in ROUTES:
                if route[0] == 1 and (route[4] > 2) == far:
                    arrive(1, route[1], route[2], route[4])
            if far:
                accum(rf, others, None, 3, 3, True)
            else:
                accum(rf, others, None, 6, 5)

    own = pl.ds(base(0), sh)
    inv = 1.0 / rows_all

    acc[...] = jnp.zeros_like(acc)
    pltpu.make_async_copy(g_hbm, gv, load_sem.at[n_z]).wait()
    accum(gv, (), loaded, None)
    tot = plane_sum(0)
    w0, rr0 = tot[:rows], tot[rows:rows + 1]
    pp0 = rr0
    a0 = []

    def residual1(c, s):
        if c is None:
            a0.append(rr0 / (z_finish(0) * inv + DAMPING * pp0))
            return
        at = span(0, c)
        r1f[at, :] = gv[at, :] - a0[0] * (s * inv + DAMPING * gv[at, :])

    exchange(0, t1, w0, r1f, (gv,), lambda: z_start(0, w0), residual1)

    tot = plane_sum(1)
    rr1, rp1 = tot[rows:rows + 1], tot[rows + 1:rows + 2]
    b0 = rr1 / rr0
    u1 = tot[:rows]
    w1 = u1 + b0 * w0
    pp1 = rr1 + b0 * (2.0 * rp1 + b0 * pp0)
    a1 = []

    def residual2(c, s):
        if c is None:
            a1.append(rr1 / (z_finish(1) * inv + DAMPING * pp1))
            return
        at = span(0, c)
        p1 = r1f[at, :] + b0 * gv[at, :]
        r2f[at, :] = r1f[at, :] - a1[0] * ((s + b0 * t1[at, :]) * inv + DAMPING * p1)

    exchange(1, t2, u1, r2f, (gv, r1f), lambda: z_start(1, w1), residual2)

    tot = plane_sum(2)
    rr2, rg2, rq2 = tot[rows:rows + 1], tot[rows + 1:rows + 2], tot[rows + 2:rows + 3]
    b1 = rr2 / rr1
    w2 = tot[:rows] + b1 * w1
    pp2 = rr2 + b1 * (2.0 * (rq2 + b0 * rg2) + b1 * pp1)
    z_start(2, w2)
    p1 = r1f[own, :] + b0 * gv[own, :]
    x1 = a0[0] * gv[own, :] + a1[0] * p1
    p2 = r2f[own, :] + b1 * p1
    a2 = rr2 / (z_finish(2) * inv + DAMPING * pp2)
    x_ref[...] = x1 + a2 * p2

    sent = pl.ds(0, (n_z - 1) * sh)
    for it in range(2):
        for phase, ref in enumerate(((t1, t2)[it], (r1f, r2f)[it])):
            every = ref.at[sent, :]
            pltpu.make_async_copy(every, every, ring_send.at[it, phase]).wait()
    for it in range(3):
        every = gath.at[it, pl.ds(0, n_p - 1)]
        pltpu.make_async_copy(every, every, pl_send.at[it]).wait()
        every = zgath.at[it, pl.ds(0, n_z - 1)]
        pltpu.make_async_copy(every, every, z_send.at[it]).wait()


def body(derivs, gradient):
    n_p, n_z = lax.axis_size("param"), lax.axis_size("walker")
    rows, cols = derivs.shape
    tiles = cols // LANES
    sh = tiles // n_z
    cuts = tuple((sh // 8 * c + PIECES - 1) // PIECES * 8 for c in range(PIECES + 1))
    d = derivs.reshape(rows, tiles, LANES).transpose(1, 0, 2)
    g = gradient.reshape(tiles, LANES)
    f32 = jnp.float32
    full = pltpu.VMEM((tiles, LANES), f32)
    x = pl.pallas_call(
        functools.partial(kernel, (n_p, n_z, rows, sh, cuts, rows * n_z)),
        out_shape=jax.ShapeDtypeStruct((sh, LANES), f32),
        in_specs=[pl.BlockSpec(memory_space=pltpu.HBM)] * 2,
        out_specs=pl.BlockSpec(memory_space=pltpu.VMEM),
        scratch_shapes=[
            pltpu.VMEM((rows, tiles, LANES), f32),
            full, full, full, full, full,
            pltpu.VMEM((2, 2, 4, sh, LANES), f32),
            pltpu.VMEM((16, 8, LANES), f32),
            pltpu.VMEM((3, 1, LANES), f32),
            pltpu.VMEM((3, n_p, 1, LANES), f32),
            pltpu.VMEM((3, 1, LANES), f32),
            pltpu.VMEM((3, n_z, 1, LANES), f32),
            pltpu.SemaphoreType.DMA((n_z + 1,)),
            pltpu.SemaphoreType.DMA((2, 2)),
            pltpu.SemaphoreType.DMA((2, 2, 2, 4, PIECES)),
            pltpu.SemaphoreType.DMA((3,)),
            pltpu.SemaphoreType.DMA((3,)),
            pltpu.SemaphoreType.DMA((3,)),
            pltpu.SemaphoreType.DMA((3,)),
        ],
        compiler_params=pltpu.CompilerParams(
            collective_id=0, has_side_effects=True, vmem_limit_bytes=56 * 1024 * 1024),
        name="cg_solve",
    )(d, g)
    return x.reshape(sh * LANES)


def solution(mesh):
    in_specs = (P("walker", "param"), P("param"))
    out_specs = P(("param", "walker"))
    return jax.shard_map(body, mesh=mesh, in_specs=in_specs, out_specs=out_specs, check_vma=False)
```

```python
import functools
import itertools

import jax
import jax.numpy as jnp
from jax import lax
from jax.experimental import pallas as pl
from jax.experimental.pallas import tpu as pltpu
from jax.sharding import PartitionSpec as P

DAMPING = 0.001
PIECES = 4
ROUTES = (
    (0, 0, 0, 4, 3), (0, 0, 1, 3, 2), (0, 0, 0, 2, 1), (0, 1, 1, 4, 3), (0, 1, 0, 3, 2), (0, 1, 1, 2, 1),
    (0, 2, 1, 4, 3), (0, 2, 0, 3, 2), (0, 2, 1, 2, 1), (0, 3, 0, 4, 3), (0, 3, 1, 3, 2), (0, 3, 0, 2, 1),
    (0, 0, 1, 1, 0), (0, 1, 0, 1, 0), (0, 3, 1, 1, 0), (0, 0, 0, 3, 0), (0, 0, 1, 2, 0), (0, 0, 0, 1, 0),
    (0, 1, 1, 3, 0), (0, 1, 0, 2, 0), (0, 2, 0, 1, 0), (0, 1, 1, 1, 0), (0, 2, 0, 2, 0), (0, 2, 1, 3, 0),
    (0, 3, 0, 3, 0), (0, 2, 1, 1, 0), (0, 3, 0, 1, 0), (0, 3, 1, 2, 0), (1, 0, 0, 0, 2), (1, 0, 0, 0, 1),
    (1, 0, 1, 0, 2), (1, 0, 1, 0, 1), (1, 1, 0, 0, 2), (1, 1, 1, 0, 2), (1, 2, 0, 0, 2), (1, 2, 1, 0, 2),
    (1, 3, 0, 0, 2), (1, 3, 1, 0, 2), (1, 0, 0, 2, 4), (1, 0, 0, 2, 3), (1, 0, 1, 2, 3), (1, 1, 0, 0, 1),
    (1, 1, 1, 0, 1), (1, 1, 0, 2, 3), (1, 1, 1, 2, 4), (1, 1, 1, 2, 3), (1, 2, 0, 0, 1), (1, 2, 1, 0, 1),
    (1, 2, 0, 2, 3), (1, 2, 1, 2, 4), (1, 2, 1, 2, 3), (1, 3, 0, 0, 1), (1, 3, 1, 0, 1), (1, 3, 0, 2, 4),
    (1, 3, 0, 2, 3), (1, 3, 1, 2, 3),
)
LANES = 128
MESH = pl.DeviceIdType.MESH


def kernel(cfg, d_hbm, g_hbm, x_ref, dv, gv, t1, t2, r1f, r2f, rb, acc,
           msg, gath, zmsg, zgath,
           load_sem, ring_send, ring_recv, pl_send, pl_recv, z_send, z_recv):
    n_p, n_z, rows, sh, cuts, rows_all = cfg
    me_p = lax.axis_index("param")
    me_z = lax.axis_index("walker")
    groups = sh // 8

    def base(k):
        return pl.multiple_of(lax.rem(me_z + (k + n_z), n_z) * sh, 8)

    y, x, core = me_p // 8, lax.rem(me_p // 2, 4), lax.rem(me_p, 2)
    ys, xs, cores = ([lax.rem(at + i, n) for i in range(n)] for at, n in ((y, 4), (x, 4), (core, 2)))
    plane = [(ys[j] * 4 + xs[i]) * 2 + cores[k]
             for j, i, k in sorted(itertools.product(range(4), range(4), range(2)),
                                   key=lambda s: -min(s[0], 4 - s[0]) - min(s[1], 4 - s[1]) - 0.1 * s[2])
             if (j, i, k) != (0, 0, 0)]

    barrier = pltpu.get_barrier_semaphore()

    def greet_z(i, c):
        pl.semaphore_signal(barrier, inc=1, device_id={"walker": lax.rem(me_z + i, n_z)}, device_id_type=MESH)
        return c

    pltpu.make_async_copy(g_hbm, gv, load_sem.at[n_z]).start()
    for k in range(n_z):
        if k == 1:
            for peer in plane:
                pl.semaphore_signal(barrier, inc=1, device_id={"param": peer}, device_id_type=MESH)
            lax.fori_loop(1, n_z, greet_z, 0)
        at = pl.ds(k * sh, sh)
        for r in range(rows):
            pltpu.make_async_copy(d_hbm.at[at, r, :], dv.at[r, at, :], load_sem.at[k]).start()

    def loaded(k):
        part = dv.at[:, pl.ds(pl.multiple_of(k * sh, 8), sh), :]
        pltpu.make_async_copy(part, part, load_sem.at[k]).wait()

    def accum(vec, others, ready=None, first=0, count=None, more=False):
        n = rows + 1 + len(others)

        def shard(k, a):
            if ready is not None:
                ready(k)
            b = k * sh if first is None else pl.multiple_of(lax.rem(me_z + (first + k), n_z) * sh, 8)
            out = list(a)
            for i in range(groups):
                o = pl.multiple_of(b + i * 8, 8)
                v = vec[pl.ds(o, 8), :]
                for r in range(rows):
                    out[r] = out[r] + dv[r, pl.ds(o, 8), :] * v
                out[rows] = out[rows] + v * v
                for j, ref in enumerate(others):
                    out[rows + 1 + j] = out[rows + 1 + j] + ref[pl.ds(o, 8), :] * v
            return tuple(out)

        init = tuple(acc[i] if more else jnp.zeros((8, LANES), jnp.float32) for i in range(n))
        a = lax.fori_loop(0, n_z if count is None else count, shard, init)
        for i in range(n):
            acc[i] = a[i]

    sub = lax.broadcasted_iota(jnp.int32, (16, LANES), 0)
    lane = lax.broadcasted_iota(jnp.int32, (16, LANES), 1)
    diag = sub == lane

    def plane_sum(it):
        part = jnp.sum(acc[...], axis=1)
        part = jnp.sum(part, axis=1, keepdims=True)
        row = jnp.sum(jnp.where(diag, part, 0.0), axis=0, keepdims=True)
        msg[it] = row
        gath[it, me_p] = row
        if it == 0:
            pl.semaphore_wait(barrier, n_p - 1 + n_z - 1)

        for peer in plane:
            pltpu.make_async_remote_copy(msg.at[it], gath.at[it, me_p], pl_send.at[it], pl_recv.at[it],
                                         device_id={"param": peer}, device_id_type=MESH).start()
        every = gath.at[it, pl.ds(0, n_p - 1)]
        pltpu.make_async_copy(every, every, pl_recv.at[it]).wait()
        tot = jnp.sum(gath[it, :, 0, :], axis=0, keepdims=True)
        tot = jnp.sum(jnp.where(diag, tot, 0.0), axis=1, keepdims=True)
        return jnp.broadcast_to(tot, (16, LANES))

    def z_start(it, w):
        row = jnp.sum(w * w, axis=0, keepdims=True)
        zmsg[it] = row
        zgath[it, me_z] = row

        def send(i, c):
            peer = lax.rem(me_z + i, n_z)
            pltpu.make_async_remote_copy(zmsg.at[it], zgath.at[it, me_z], z_send.at[it], z_recv.at[it],
                                         device_id={"walker": peer}, device_id_type=MESH).start()
            return c

        lax.fori_loop(1, n_z, send, 0)

    def z_finish(it):
        every = zgath.at[it, pl.ds(0, n_z - 1)]
        pltpu.make_async_copy(every, every, z_recv.at[it]).wait()
        return jnp.sum(zgath[it, :, 0, :], axis=0, keepdims=True)

    def project(first, count, t, wv):
        def shard(k, c):
            b = base(first + k)
            for i in range(groups):
                o = pl.multiple_of(b + i * 8, 8)
                s = dv[0, pl.ds(o, 8), :] * wv[0]
                for r in range(1, rows):
                    s = s + dv[r, pl.ds(o, 8), :] * wv[r]
                t[pl.ds(o, 8), :] = s
            return c

        lax.fori_loop(0, count, shard, 0)

    pieces = tuple((cuts[c], cuts[c + 1] - cuts[c]) for c in range(len(cuts) - 1))
    signs = (1, -1)

    def span(k, c):
        lo, n = pieces[c]
        return pl.ds(pl.multiple_of(base(k) + lo, 8), n)

    def exchange(it, t, w, rf, others, meanwhile, finish):
        wv = [jnp.broadcast_to(w[r:r + 1, :], (8, LANES)) for r in range(rows)]

        def copy(phase, c, way, a, b):
            lo, n = pieces[c]
            sign = signs[way]
            if phase == 0:
                src, dst = t.at[span(sign * a, c), :], rb.at[it, way, a - 1, pl.ds(lo, n), :]
                slot = a - 1
            else:
                src = dst = rf.at[span(-sign * a, c), :]
                slot = b - 1
            peer = lax.rem(me_z + (n_z + sign * abs(a - b)), n_z)
            return pltpu.make_async_remote_copy(
                src, dst, ring_send.at[it, phase], ring_recv.at[it, phase, way, slot, c],
                device_id={"walker": peer}, device_id_type=MESH)

        def arrive(phase, c, way, at):
            total = None
            for route in ROUTES:
                if route[:3] == (phase, c, way) and route[4] == at and route not in waited:
                    waited.add(route)
                    copy(*route).wait_recv()
                    if phase == 0:
                        lo, n = pieces[c]
                        part = rb[it, way, route[3] - 1, pl.ds(lo, n), :]
                        total = part if total is None else total + part
            return total

        waited, done = set(), set()
        project(3, 3, t, wv)
        for phase, c, way, a, b in ROUTES:
            if phase == 0:
                if a < 3 and "rest" not in done:
                    project(6, 5, t, wv)
                    done.add("rest")
                s = arrive(0, c, way, a)
                if s is not None:
                    t[span(signs[way] * a, c), :] += s
            elif a == 0:
                if c not in done:
                    if "scale" not in done:
                        finish(None, None)
                        done.add("scale")
                    s = t[span(0, c), :]
                    for w_ in range(2):
                        s = s + arrive(0, c, w_, 0)
                    t[span(0, c), :] = s
                    finish(c, s)
                    done.add(c)
            else:
                arrive(1, c, way, a)
            copy(phase, c, way, a, b).start()
            if "z" not in done and "rest" in done:
                meanwhile()
                done.add("z")
        for far in (False, True):
            for route in ROUTES:
                if route[0] == 1 and (route[4] > 2) == far:
                    arrive(1, route[1], route[2], route[4])
            if far:
                accum(rf, others, None, 3, 3, True)
            else:
                accum(rf, others, None, 6, 5)

    own = pl.ds(base(0), sh)
    inv = 1.0 / rows_all

    acc[...] = jnp.zeros_like(acc)
    pltpu.make_async_copy(g_hbm, gv, load_sem.at[n_z]).wait()
    accum(gv, (), loaded, None)
    tot = plane_sum(0)
    w0, rr0 = tot[:rows], tot[rows:rows + 1]
    pp0 = rr0
    a0 = []

    def residual1(c, s):
        if c is None:
            a0.append(rr0 / (z_finish(0) * inv + DAMPING * pp0))
            return
        at = span(0, c)
        r1f[at, :] = gv[at, :] - a0[0] * (s * inv + DAMPING * gv[at, :])

    exchange(0, t1, w0, r1f, (gv,), lambda: z_start(0, w0), residual1)

    tot = plane_sum(1)
    rr1, rp1 = tot[rows:rows + 1], tot[rows + 1:rows + 2]
    b0 = rr1 / rr0
    u1 = tot[:rows]
    w1 = u1 + b0 * w0
    pp1 = rr1 + b0 * (2.0 * rp1 + b0 * pp0)
    a1 = []

    def residual2(c, s):
        if c is None:
            a1.append(rr1 / (z_finish(1) * inv + DAMPING * pp1))
            return
        at = span(0, c)
        p1 = r1f[at, :] + b0 * gv[at, :]
        r2f[at, :] = r1f[at, :] - a1[0] * ((s + b0 * t1[at, :]) * inv + DAMPING * p1)

    exchange(1, t2, u1, r2f, (gv, r1f), lambda: z_start(1, w1), residual2)

    tot = plane_sum(2)
    rr2, rg2, rq2 = tot[rows:rows + 1], tot[rows + 1:rows + 2], tot[rows + 2:rows + 3]
    b1 = rr2 / rr1
    w2 = tot[:rows] + b1 * w1
    pp2 = rr2 + b1 * (2.0 * (rq2 + b0 * rg2) + b1 * pp1)
    z_start(2, w2)
    p1 = r1f[own, :] + b0 * gv[own, :]
    x1 = a0[0] * gv[own, :] + a1[0] * p1
    p2 = r2f[own, :] + b1 * p1
    a2 = rr2 / (z_finish(2) * inv + DAMPING * pp2)
    x_ref[...] = x1 + a2 * p2

    sent = pl.ds(0, (n_z - 1) * sh)
    for it in range(2):
        for phase, ref in enumerate(((t1, t2)[it], (r1f, r2f)[it])):
            every = ref.at[sent, :]
            pltpu.make_async_copy(every, every, ring_send.at[it, phase]).wait()
    for it in range(3):
        every = gath.at[it, pl.ds(0, n_p - 1)]
        pltpu.make_async_copy(every, every, pl_send.at[it]).wait()
        every = zgath.at[it, pl.ds(0, n_z - 1)]
        pltpu.make_async_copy(every, every, z_send.at[it]).wait()


def body(derivs, gradient):
    n_p, n_z = lax.axis_size("param"), lax.axis_size("walker")
    rows, cols = derivs.shape
    tiles = cols // LANES
    sh = tiles // n_z
    cuts = tuple((sh // 8 * c + PIECES - 1) // PIECES * 8 for c in range(PIECES + 1))
    d = derivs.reshape(rows, tiles, LANES).transpose(1, 0, 2)
    g = gradient.reshape(tiles, LANES)
    f32 = jnp.float32
    full = pltpu.VMEM((tiles, LANES), f32)
    x = pl.pallas_call(
        functools.partial(kernel, (n_p, n_z, rows, sh, cuts, rows * n_z)),
        out_shape=jax.ShapeDtypeStruct((sh, LANES), f32),
        in_specs=[pl.BlockSpec(memory_space=pltpu.HBM)] * 2,
        out_specs=pl.BlockSpec(memory_space=pltpu.VMEM),
        scratch_shapes=[
            pltpu.VMEM((rows, tiles, LANES), f32),
            full, full, full, full, full,
            pltpu.VMEM((2, 2, 4, sh, LANES), f32),
            pltpu.VMEM((16, 8, LANES), f32),
            pltpu.VMEM((3, 1, LANES), f32),
            pltpu.VMEM((3, n_p, 1, LANES), f32),
            pltpu.VMEM((3, 1, LANES), f32),
            pltpu.VMEM((3, n_z, 1, LANES), f32),
            pltpu.SemaphoreType.DMA((n_z + 1,)),
            pltpu.SemaphoreType.DMA((2, 2)),
            pltpu.SemaphoreType.DMA((2, 2, 2, 4, PIECES)),
            pltpu.SemaphoreType.DMA((3,)),
            pltpu.SemaphoreType.DMA((3,)),
            pltpu.SemaphoreType.DMA((3,)),
            pltpu.SemaphoreType.DMA((3,)),
        ],
        compiler_params=pltpu.CompilerParams(
            collective_id=0, has_side_effects=True, vmem_limit_bytes=56 * 1024 * 1024),
        name="cg_solve",
    )(d, g)
    return x.reshape(sh * LANES)


def solution(mesh):
    in_specs = (P("walker", "param"), P("param"))
    out_specs = P(("param", "walker"))
    return jax.shard_map(body, mesh=mesh, in_specs=in_specs, out_specs=out_specs, check_vma=False)
```
